32 devices in a mesh: groups: 2 (over y), ctx: 4 (over z), head: 2 (over x), sub: 2 (over core).
Axes of the slice: x: 2, y: 2, z: 4, core: 2. Of those that a mesh axis runs over, the one named last changes fastest.
Arguments:
- queries: bfloat16 [3072, 8192], P(('groups', 'ctx'), ('head', 'sub')), parts along dimension 0, may hold values from -60 to 60
- key_rows: bfloat16 [3072, 1024], P(('groups', 'ctx'), 'head'), parts along dimension 0, may hold values from -6 to 6
- value_rows: bfloat16 [3072, 1024], P(('groups', 'ctx'), 'head'), parts along dimension 0, may hold values from -6 to 6
- out_weight: bfloat16 [8192, 5120], P(('head', 'sub'), 'ctx'), may hold values from -0.375 to 0.375
Outputs:
- mixed: bfloat16 [3072, 5120], P(('groups', 'ctx'), ('head', 'sub')), parts along dimension 0
The draws below stay inside these ranges and needn't reach their ends.
There are 2 independent parts, one for each index of `groups`. The reference program is written for one: setup_inputs(seed, part) draws one part's arguments, and reference() takes and returns one part's arrays. A program takes and returns all parts, laid end to end along the dimension named above; an argument that names none is the same for every part. Nothing has to cross between parts.
All inputs are finite; a program needn't handle non-finite values.
Results may differ from the reference program's by a relative error of at most 0.02.
Values may be sent and summed in bfloat16 or wider, within the bound.
A program may use at most 128 MiB of HBM per device.

```python
import jax
import jax.numpy as jnp
from jax import lax

D = 5120
QH = 64
KVH = 8
HD = 128
TOKENS = 1536
QPD = 16
N_HEAD = 2
N_SUB = 2


def paired_draw(key):
    key_base = jax.random.fold_in(key, 701)
    query_base = jax.random.fold_in(key, 702)
    keys_out = jnp.clip(jax.random.normal(key_base, (TOKENS, KVH * HD), jnp.float32), -6.0, 6.0)
    queries_out = 1.5 * jnp.clip(jax.random.normal(query_base, (TOKENS, QH * HD), jnp.float32), -6.0, 6.0)
    return (queries_out, keys_out)


def draw_queries(key, part):
    return paired_draw(key)[0].astype(jnp.bfloat16)


def draw_key_rows(key, part):
    return paired_draw(key)[1].astype(jnp.bfloat16)


def steps_of(rng, extent, split, least, high):
    level, own = 1.0, jax.random.fold_in(rng, 6)
    for dim, blocks in split:
        steps = jnp.exp(jax.random.uniform(jax.random.fold_in(own, dim), (blocks,), jnp.float32, least / len(split), high / len(split)))
        level = level * jnp.repeat(steps, extent[dim] // blocks).reshape([-1 if axis == dim else 1 for axis in range(len(extent))])
    return level


def noise(key, shape, spread, most, pieces=(), kind=jnp.bfloat16):
    level = steps_of(key, shape, pieces, -0.22, 0.18) if pieces else 1.0
    values = jax.random.normal(key, shape, jnp.float32) * spread * level
    return jnp.minimum(jnp.maximum(values, -most), most).astype(kind)


def setup_inputs(seed: int = 0, part: int = 0) -> dict:
    splits = jax.random.split(jax.random.key(seed), 5)
    part_splits = jax.random.split(jax.random.fold_in(splits[4], part), 5)
    return {
        "queries": draw_queries(jax.random.fold_in(jax.random.fold_in(splits[4], part), 71), part),
        "key_rows": draw_key_rows(jax.random.fold_in(jax.random.fold_in(splits[4], part), 71), part),
        "value_rows": noise(part_splits[2], (TOKENS, KVH * HD), 1.0, 6.0, ((0, 4), (1, 2))),
        "out_weight": noise(splits[3], (QH * HD, D), (QH * HD // 32) ** -0.5, 0.375, ((0, 4), (1, 4))),
    }


def reference(queries, key_rows, value_rows, out_weight):
    group_ratio = QH // KVH
    query_heads = queries.reshape(TOKENS, QH, HD)
    key_heads = key_rows.reshape(TOKENS, KVH, HD)
    value_heads = value_rows.reshape(TOKENS, KVH, HD)
    factor = 1.0 / (HD ** 0.5)

    def one_head(head_id):
        kv_id = head_id // group_ratio
        q_head = lax.dynamic_index_in_dim(query_heads, head_id, 1, keepdims=False)
        k_head = lax.dynamic_index_in_dim(key_heads, kv_id, 1, keepdims=False)
        v_head = lax.dynamic_index_in_dim(value_heads, kv_id, 1, keepdims=False)
        scores = jnp.dot(q_head, k_head.T, preferred_element_type=jnp.float32) * factor
        row_max = jnp.max(scores, axis=1, keepdims=True)
        expo = jnp.exp(scores - row_max)
        weights = expo.astype(jnp.bfloat16)
        summed = jnp.dot(weights, v_head, preferred_element_type=jnp.float32)
        return (summed / jnp.sum(expo, axis=1, keepdims=True)).astype(jnp.bfloat16)

    per_head = lax.map(one_head, jnp.arange(QH, dtype=jnp.int32))
    attended = jnp.transpose(per_head, (1, 0, 2)).reshape(TOKENS, QH * HD)
    width = QPD * HD

    def add_group(total, group_id):
        offset = (group_id * width).astype(jnp.int32)
        cols = lax.dynamic_slice_in_dim(attended, offset, width, 1)
        rows = lax.dynamic_slice_in_dim(out_weight, offset, width, 0)
        partial_value = jnp.dot(cols, rows, preferred_element_type=jnp.float32).astype(jnp.bfloat16)
        return total + partial_value.astype(jnp.float32), None

    total, _ = lax.scan(add_group, jnp.zeros((TOKENS, D), jnp.float32), jnp.arange(N_HEAD * N_SUB, dtype=jnp.int32))
    return total.astype(jnp.bfloat16)
```

```python
import functools
import math

import jax
import jax.numpy as jnp
from jax import lax
from jax.experimental import pallas as pl
from jax.experimental.pallas import tpu as pltpu
from jax.sharding import PartitionSpec as P

QH = 64
KVH = 8
HD = 128
CHUNKS = 2
ROWS = 128


def attend_kernel(q_ref, k_ref, v_ref, o_ref, v_ext):
    v_ext[:, :HD] = v_ref[...]
    v_ext[:, HD:] = jnp.ones((v_ref.shape[0], HD), v_ref.dtype)
    factor = math.log2(math.e) / HD**0.5
    for start in range(0, q_ref.shape[0], ROWS):
        rows = pl.ds(start, ROWS)
        scores = lax.dot_general(
            q_ref[rows, :], k_ref[...], (((1,), (1,)), ((), ())), preferred_element_type=jnp.float32
        )
        row_max = jnp.max(scores, axis=1, keepdims=True)
        weights = jnp.exp2((scores - row_max) * factor).astype(jnp.bfloat16)
        both = jnp.dot(weights, v_ext[...], preferred_element_type=jnp.float32)
        o_ref[rows, :] = (both[:, :HD] / both[:, HD:]).astype(o_ref.dtype)


def attend(queries, key_value, first_head, heads, per_pair, pairs):
    tokens = queries.shape[0]
    keys = key_value.shape[0]
    return pl.pallas_call(
        attend_kernel,
        grid=(heads,),
        out_shape=jax.ShapeDtypeStruct((tokens, heads * HD), jnp.bfloat16),
        in_specs=[
            pl.BlockSpec((tokens, HD), lambda h: (0, first_head + h)),
            pl.BlockSpec((keys, HD), lambda h: (0, (first_head + h) // per_pair)),
            pl.BlockSpec((keys, HD), lambda h: (0, pairs + (first_head + h) // per_pair)),
        ],
        out_specs=pl.BlockSpec((tokens, HD), lambda h: (0, h)),
        scratch_shapes=[pltpu.VMEM((keys, 2 * HD), jnp.bfloat16)],
        compiler_params=pltpu.CompilerParams(vmem_limit_bytes=48 * 2**20),
        cost_estimate=pl.CostEstimate(
            flops=8 * heads * tokens * keys * HD,
            bytes_accessed=4 * tokens * heads * HD + 4 * keys * HD,
            transcendentals=heads * tokens * keys,
        ),
    )(queries, key_value, key_value)


def on_device(queries, key_rows, value_rows, out_weight):
    token_count = queries.shape[0]
    heads_here = queries.shape[1] // HD
    group_ratio = QH // KVH
    pairs_read = max(heads_here // group_ratio, 1)
    per_pair = heads_here // pairs_read
    head_offset = lax.axis_index("sub") * heads_here // group_ratio
    key_value = jnp.concatenate(
        [
            lax.dynamic_slice_in_dim(rows, head_offset * HD, pairs_read * HD, 1)
            for rows in (key_rows, value_rows)
        ],
        axis=1,
    )
    key_value = lax.all_gather(key_value, "ctx", axis=0, tiled=True)
    heads = heads_here // CHUNKS
    partial_value = None
    for chunk in range(CHUNKS):
        attended = attend(queries, key_value, chunk * heads, heads, per_pair, pairs_read)
        everyone = lax.all_gather(attended, "ctx", axis=0, tiled=True)
        rows = out_weight[chunk * heads * HD : (chunk + 1) * heads * HD]
        added = jnp.dot(everyone, rows, preferred_element_type=jnp.float32)
        partial_value = added if partial_value is None else partial_value + added
    summed = lax.psum_scatter(
        partial_value.astype(jnp.bfloat16), ("head", "sub"), scatter_dimension=0, tiled=True
    )
    size = lax.axis_size("ctx")
    route = [(a * size + b, b * size + a) for a in range(size) for b in range(size)]
    return lax.ppermute(summed, ("ctx", "head", "sub"), route)


def solution(mesh):
    assert mesh.shape["ctx"] == mesh.shape["head"] * mesh.shape["sub"]
    return jax.shard_map(
        on_device,
        mesh=mesh,
        in_specs=(
            P(("groups", "ctx"), ("head", "sub")),
            P(("groups", "ctx"), "head"),
            P(("groups", "ctx"), "head"),
            P(("head", "sub"), "ctx"),
        ),
        out_specs=P(("groups", "ctx"), ("head", "sub")),
        check_vma=False,
    )
```

```python
import functools
import math

import jax
import jax.numpy as jnp
from jax import lax
from jax.experimental import pallas as pl
from jax.experimental.pallas import tpu as pltpu
from jax.sharding import PartitionSpec as P

QH = 64
KVH = 8
HD = 128
CHUNKS = 4
ROWS = 128
MESH = pl.DeviceIdType.MESH


def kernel(
    n, n_head, per_pair, pairs, kv_ref, q_ref, w_hbm, o_ref,
    kv_all, v_ext, att, w, own, out, rx1, summed, rx2, final,
    w_sem, kv_send, kv_recv, a_send, a_recv, s1, r1, s2, r2, s3, r3,
):
    me, head, sub = (lax.axis_index(a) for a in ("ctx", "head", "sub"))
    other = 1 - sub
    hs = head * 2 + sub
    tokens, width = q_ref.shape
    heads = width // HD
    columns = w.shape[1]
    piece = width // CHUNKS
    to_right, to_left = me < n - 1, me > 0
    right, left = lax.min(me + 1, n - 1), lax.max(me - 1, 0)
    away = hs != me
    turned = {"ctx": hs, "head": me // 2, "sub": me % 2}

    load_w = pltpu.make_async_copy(w_hbm, w, w_sem)
    load_w.start()

    barrier = pltpu.get_barrier_semaphore()

    def greet(where):
        pl.semaphore_signal(barrier, inc=1, device_id=where, device_id_type=MESH)

    pl.when(to_right)(lambda: greet({"ctx": right}))
    pl.when(to_left)(lambda: greet({"ctx": left}))
    pl.when(away)(lambda: greet(turned))
    greet({"sub": other})
    for step in range(1, n_head):
        greet({"head": lax.rem(head + step, n_head)})
    count = n_head + to_right.astype(jnp.int32) + to_left.astype(jnp.int32)
    pl.semaphore_wait(barrier, count + away.astype(jnp.int32))

    def remote(src, dst, send, recv, where):
        return pltpu.make_async_remote_copy(
            src_ref=src, dst_ref=dst, send_sem=send, recv_sem=recv, device_id=where, device_id_type=MESH
        )

    def rows_of(b):
        return pl.ds(pl.multiple_of(b * tokens, tokens), tokens)

    def kv_copy(src, b, way, d):
        where = {"ctx": right if way == 0 else left}
        return remote(src, kv_all.at[rows_of(b)], kv_send.at[way, d], kv_recv.at[b], where)

    pl.when(to_right)(lambda: kv_copy(kv_ref, me, 0, 0).start())
    pl.when(to_left)(lambda: kv_copy(kv_ref, me, 1, 0).start())
    kv_all[rows_of(me), :] = kv_ref[...]

    @pl.loop(1, n)
    def _(d):
        @pl.when(me - d >= 0)
        def _():
            copy = kv_copy(kv_all.at[rows_of(me - d)], me - d, 0, d)
            copy.wait_recv()
            pl.when(to_right)(lambda: copy.start())

        @pl.when(me + d < n)
        def _():
            copy = kv_copy(kv_all.at[rows_of(me + d)], me + d, 1, d)
            copy.wait_recv()
            pl.when(to_left)(lambda: copy.start())

    for p in range(pairs):
        v_ext[p, :, :HD] = kv_all[:, (pairs + p) * HD : (pairs + p + 1) * HD]
        v_ext[p, :, HD:] = jnp.ones((v_ext.shape[1], HD), v_ext.dtype)

    def a_copy(b, j, way, d):
        where = {"ctx": right if way == 0 else left}
        part = att.at[b, :, pl.ds(j * piece, piece)]
        return remote(part, part, a_send.at[way, d, j], a_recv.at[b, j], where)

    factor = math.log2(math.e) / HD**0.5
    for j in range(CHUNKS):

        @pl.loop(j * heads // CHUNKS, (j + 1) * heads // CHUNKS)
        def _(h):
            pair = h // per_pair
            cols = pl.ds(pl.multiple_of(h * HD, HD), HD)
            keys = kv_all[:, pl.ds(pl.multiple_of(pair * HD, HD), HD)]
            for start in range(0, tokens, ROWS):
                rows = pl.ds(start, ROWS)
                scores = lax.dot_general(
                    q_ref[rows, cols], keys, (((1,), (1,)), ((), ())), preferred_element_type=jnp.float32
                )
                row_max = jnp.max(scores, axis=1, keepdims=True)
                weights = jnp.exp2((scores - row_max) * factor).astype(jnp.bfloat16)
                both = jnp.dot(weights, v_ext[pair], preferred_element_type=jnp.float32)
                att[me, rows, cols] = (both[:, :HD] / both[:, HD:]).astype(att.dtype)

        pl.when(to_right)(lambda: a_copy(me, j, 0, 0).start())
        pl.when(to_left)(lambda: a_copy(me, j, 1, 0).start())

    load_w.wait()
    tile = 256 if columns % 256 == 0 else columns

    def product(t, dst):
        if tile == columns:
            dst[...] = jnp.dot(att[t], w[...], preferred_element_type=jnp.float32).astype(dst.dtype)
        else:

            @pl.loop(0, columns // tile)
            def _(c):
                cols = pl.ds(pl.multiple_of(c * tile, tile), tile)
                dst[:, cols] = jnp.dot(
                    att[t], w[:, cols], preferred_element_type=jnp.float32
                ).astype(dst.dtype)

    def core_copy(g):
        return remote(out.at[g], rx1.at[g], s1.at[g], r1.at[g], {"sub": other})

    def head_copy(g):
        return remote(summed.at[g], rx2.at[head], s2.at[g], r2.at[head], {"head": g})

    def last_copy():
        return remote(final, o_ref, s3, r3, turned)

    def multiply(t):
        g = t // 2

        @pl.when(t % 2 == sub)
        def _():
            product(t, own.at[g])

        @pl.when(t % 2 != sub)
        def _():
            product(t, out.at[g])
            core_copy(g).start()

    def combine(t):
        g = t // 2

        @pl.when(t % 2 == sub)
        def _():
            core_copy(g).wait_recv()
            summed[g] = (own[g].astype(jnp.float32) + rx1[g].astype(jnp.float32)).astype(summed.dtype)
            pl.when(g != head)(lambda: head_copy(g).start())

    def finish():
        for step in range(1, n_head):
            source = lax.rem(head + step, n_head)
            remote(
                summed.at[source], rx2.at[source], s2.at[source], r2.at[source], {"head": source}
            ).wait_recv()
        for start in range(0, tokens, ROWS):
            rows = pl.ds(start, ROWS)
            total = summed[head, rows, :].astype(jnp.float32)
            for step in range(1, n_head):
                total += rx2[lax.rem(head + step, n_head), rows, :].astype(jnp.float32)
            final[rows, :] = total.astype(final.dtype)
        pl.when(away)(lambda: last_copy().start())

    multiply(me)
    combine(me)
    gap = lax.max(hs - me, me - hs)

    @pl.loop(1, n)
    def _(d):
        for j in range(CHUNKS):

            @pl.when(me - d >= 0)
            def _():
                copy = a_copy(me - d, j, 0, d)
                copy.wait_recv()
                pl.when(to_right)(lambda: copy.start())

            @pl.when(me + d < n)
            def _():
                copy = a_copy(me + d, j, 1, d)
                copy.wait_recv()
                pl.when(to_left)(lambda: copy.start())

        pl.when(me - d >= 0)(lambda: multiply(me - d))
        pl.when(me + d < n)(lambda: multiply(me + d))
        pl.when(me - d >= 0)(lambda: combine(me - d))
        pl.when(me + d < n)(lambda: combine(me + d))
        pl.when(gap == d - 1)(finish)

    pl.when(gap == n - 1)(finish)

    @pl.when(away)
    def _():
        last_copy().wait()

    @pl.when(jnp.logical_not(away))
    def _():
        o_ref[...] = final[...]

    @pl.loop(0, n)
    def _(d):
        for way, fits, go in ((0, me - d >= 0, to_right), (1, me + d < n, to_left)):
            b = me - d if way == 0 else me + d

            @pl.when(jnp.logical_and(fits, go))
            def _():
                kv_copy(kv_all.at[rows_of(b)], b, way, d).wait_send()
                for j in range(CHUNKS):
                    a_copy(b, j, way, d).wait_send()

    @pl.loop(0, n // 2)
    def _(g):
        core_copy(g).wait_send()
        pl.when(g != head)(lambda: head_copy(g).wait_send())


def on_device(queries, key_rows, value_rows, out_weight):
    tokens, width = queries.shape
    heads_here = width // HD
    group_ratio = QH // KVH
    pairs = max(heads_here // group_ratio, 1)
    per_pair = heads_here // pairs
    head_offset = lax.axis_index("sub") * heads_here // group_ratio
    key_value = jnp.concatenate(
        [
            lax.dynamic_slice_in_dim(rows, head_offset * HD, pairs * HD, 1)
            for rows in (key_rows, value_rows)
        ],
        axis=1,
    )
    n = lax.axis_size("ctx")
    n_head = lax.axis_size("head")
    columns = out_weight.shape[1]
    block = (tokens, columns)
    groups = (n // 2,) + block
    vmem = pl.BlockSpec(memory_space=pltpu.VMEM)
    dma = pltpu.SemaphoreType.DMA
    bf16 = jnp.bfloat16
    return pl.pallas_call(
        functools.partial(kernel, n, n_head, per_pair, pairs),
        out_shape=jax.ShapeDtypeStruct(block, bf16),
        in_specs=[vmem, vmem, pl.BlockSpec(memory_space=pl.ANY)],
        out_specs=vmem,
        scratch_shapes=[
            pltpu.VMEM((n * tokens, 2 * pairs * HD), bf16),
            pltpu.VMEM((pairs, n * tokens, 2 * HD), bf16),
            pltpu.VMEM((n, tokens, width), bf16),
            pltpu.VMEM(out_weight.shape, bf16),
            pltpu.VMEM(groups, bf16),
            pltpu.VMEM(groups, bf16),
            pltpu.VMEM(groups, bf16),
            pltpu.VMEM(groups, bf16),
            pltpu.VMEM((n_head,) + block, bf16),
            pltpu.VMEM(block, bf16),
            dma,
            dma((2, n)),
            dma((n,)),
            dma((2, n, CHUNKS)),
            dma((n, CHUNKS)),
            dma((n // 2,)),
            dma((n // 2,)),
            dma((n // 2,)),
            dma((n_head,)),
            dma,
            dma,
        ],
        compiler_params=pltpu.CompilerParams(
            collective_id=0, has_side_effects=True, vmem_limit_bytes=60 * 2**20
        ),
    )(key_value, queries, out_weight)


def solution(mesh):
    assert mesh.shape["sub"] == 2
    assert mesh.shape["ctx"] == mesh.shape["head"] * mesh.shape["sub"]
    return jax.shard_map(
        on_device,
        mesh=mesh,
        in_specs=(
            P(("groups", "ctx"), ("head", "sub")),
            P(("groups", "ctx"), "head"),
            P(("groups", "ctx"), "head"),
            P(("head", "sub"), "ctx"),
        ),
        out_specs=P(("groups", "ctx"), ("head", "sub")),
        check_vma=False,
    )
```

```python
import functools
import math

import jax
import jax.numpy as jnp
from jax import lax
from jax.experimental import pallas as pl
from jax.experimental.pallas import tpu as pltpu
from jax.sharding import PartitionSpec as P

QH = 64
KVH = 8
HD = 128
CHUNKS = 8
TILE = 256
ROWS = 128
MESH = pl.DeviceIdType.MESH


def kernel(
    n, n_head, per_pair, pairs, chunks, parts, k_hbm, v_hbm, q_hbm, w_hbm, o_ref,
    kv_all, v_ext, q_ref, att, w, own, out, rx1, summed, rx2, final,
    load_sems, kv_send, kv_recv, a_send, a_recv, s1, r1, s2, r2, s3, r3,
):
    me, head, sub = (lax.axis_index(a) for a in ("ctx", "head", "sub"))
    other = 1 - sub
    hs = head * 2 + sub
    tokens, width = q_ref.shape
    heads = width // HD
    columns = w.shape[1]
    piece = width // chunks
    to_right, to_left = me < n - 1, me > 0
    right, left = lax.min(me + 1, n - 1), lax.max(me - 1, 0)
    away = hs != me
    turned = {"ctx": hs, "head": me // 2, "sub": me % 2}

    def rows_of(b):
        return pl.ds(pl.multiple_of(b * tokens, tokens), tokens)

    first = pl.multiple_of((sub * heads // (QH // KVH)) * HD, HD)
    loads = [
        pltpu.make_async_copy(
            side.at[:, pl.ds(first, pairs * HD)],
            kv_all.at[rows_of(me), pl.ds(i * pairs * HD, pairs * HD)],
            load_sems.at[i],
        )
        for i, side in enumerate((k_hbm, v_hbm))
    ]
    loads.append(pltpu.make_async_copy(q_hbm, q_ref, load_sems.at[2]))
    loads.append(pltpu.make_async_copy(w_hbm, w, load_sems.at[3]))
    for load in loads:
        load.start()

    barrier = pltpu.get_barrier_semaphore()

    def greet(where):
        pl.semaphore_signal(barrier, inc=1, device_id=where, device_id_type=MESH)

    pl.when(to_right)(lambda: greet({"ctx": right}))
    pl.when(to_left)(lambda: greet({"ctx": left}))
    pl.when(away)(lambda: greet(turned))
    greet({"sub": other})
    for step in range(1, n_head):
        greet({"head": lax.rem(head + step, n_head)})
    count = n_head + to_right.astype(jnp.int32) + to_left.astype(jnp.int32)
    pl.semaphore_wait(barrier, count + away.astype(jnp.int32))

    def remote(src, dst, send, recv, where):
        return pltpu.make_async_remote_copy(
            src_ref=src, dst_ref=dst, send_sem=send, recv_sem=recv, device_id=where, device_id_type=MESH
        )

    def kv_copy(b, way, d):
        where = {"ctx": right if way == 0 else left}
        part = kv_all.at[rows_of(b)]
        return remote(part, part, kv_send.at[way, d], kv_recv.at[b], where)

    loads[0].wait()
    loads[1].wait()
    pl.when(to_right)(lambda: kv_copy(me, 0, 0).start())
    pl.when(to_left)(lambda: kv_copy(me, 1, 0).start())

    @pl.loop(1, n)
    def _(d):
        @pl.when(me - d >= 0)
        def _():
            copy = kv_copy(me - d, 0, d)
            copy.wait_recv()
            pl.when(to_right)(lambda: copy.start())

        @pl.when(me + d < n)
        def _():
            copy = kv_copy(me + d, 1, d)
            copy.wait_recv()
            pl.when(to_left)(lambda: copy.start())

    loads[2].wait()

    def a_copy(b, j, way, d):
        where = {"ctx": right if way == 0 else left}
        part = att.at[b, :, pl.ds(j * piece, piece)]
        return remote(part, part, a_send.at[way, d, j], a_recv.at[b, j], where)

    factor = math.log2(math.e) / HD**0.5
    for j in range(chunks):
        if j % (chunks // pairs) == 0:
            p = j // (chunks // pairs)
            v_ext[p, :, :HD] = kv_all[:, (pairs + p) * HD : (pairs + p + 1) * HD]
            v_ext[p, :, HD:] = jnp.ones((v_ext.shape[1], HD), v_ext.dtype)

        @pl.loop(j * heads // chunks, (j + 1) * heads // chunks)
        def _(h):
            pair = h // per_pair
            cols = pl.ds(pl.multiple_of(h * HD, HD), HD)
            keys = kv_all[:, pl.ds(pl.multiple_of(pair * HD, HD), HD)]
            for start in range(0, tokens, ROWS):
                rows = pl.ds(start, ROWS)
                scores = lax.dot_general(
                    q_ref[rows, cols], keys, (((1,), (1,)), ((), ())), preferred_element_type=jnp.float32
                )
                row_max = jnp.max(scores, axis=1, keepdims=True)
                weights = jnp.exp2((scores - row_max) * factor).astype(jnp.bfloat16)
                both = jnp.dot(weights, v_ext[pair], preferred_element_type=jnp.float32)
                att[me, rows, cols] = (both[:, :HD] / both[:, HD:]).astype(att.dtype)

        pl.when(to_right)(lambda: a_copy(me, j, 0, 0).start())
        pl.when(to_left)(lambda: a_copy(me, j, 1, 0).start())

    loads[3].wait()
    tile = columns // parts

    def cols_of(c):
        return pl.ds(0, columns) if parts == 1 else pl.ds(pl.multiple_of(c * tile, tile), tile)

    def core_copy(g, c):
        cols = cols_of(c)
        return remote(out.at[g, :, cols], rx1.at[g, :, cols], s1.at[g, c], r1.at[g, c], {"sub": other})

    def head_copy(g, c):
        cols = cols_of(c)
        return remote(
            summed.at[g, :, cols], rx2.at[head, :, cols], s2.at[g, c], r2.at[head, c], {"head": g}
        )

    def last_copy(c):
        cols = cols_of(c)
        return remote(final.at[:, cols], o_ref.at[:, cols], s3.at[c], r3.at[c], turned)

    def product(t, c):
        cols = cols_of(c)
        return jnp.dot(att[t], w[:, cols], preferred_element_type=jnp.float32).astype(out.dtype)

    def multiply(t):
        g = t // 2

        @pl.when(t % 2 == sub)
        def _():
            @pl.loop(0, parts)
            def _(c):
                own[g, :, cols_of(c)] = product(t, c)

        @pl.when(t % 2 != sub)
        def _():
            @pl.loop(0, parts)
            def _(c):
                out[g, :, cols_of(c)] = product(t, c)
                core_copy(g, c).start()

    def combine(t):
        g = t // 2

        @pl.when(t % 2 == sub)
        def _():
            @pl.loop(0, parts)
            def _(c):
                cols = cols_of(c)
                core_copy(g, c).wait_recv()
                total = own[g, :, cols].astype(jnp.float32) + rx1[g, :, cols].astype(jnp.float32)
                summed[g, :, cols] = total.astype(summed.dtype)
                pl.when(g != head)(lambda: head_copy(g, c).start())

    def finish():
        @pl.loop(0, parts)
        def _(c):
            cols = cols_of(c)
            total = summed[head, :, cols].astype(jnp.float32)
            for step in range(1, n_head):
                source = lax.rem(head + step, n_head)
                remote(
                    summed.at[source, :, cols], rx2.at[source, :, cols],
                    s2.at[source, c], r2.at[source, c], {"head": source},
                ).wait_recv()
                total += rx2[source, :, cols].astype(jnp.float32)
            final[:, cols] = total.astype(final.dtype)
            pl.when(away)(lambda: last_copy(c).start())

    gap = lax.max(hs - me, me - hs)

    def after(d, j, last=False):
        behind, ahead = me - d + 1, me + d - 1
        if j == 0:
            pl.when(behind >= 0)(lambda: multiply(behind))
        if j == chunks // 4:
            pl.when(jnp.logical_and(ahead < n, d > 1))(lambda: multiply(ahead))
        if j == chunks // 2:
            pl.when(behind >= 0)(lambda: combine(behind))
        if j == chunks // 2 + 1:
            pl.when(jnp.logical_and(ahead < n, d > 1))(lambda: combine(ahead))
        if j == chunks - 1 and not last:
            pl.when(gap == d - 2)(finish)

    @pl.loop(1, n)
    def _(d):
        for j in range(chunks):

            @pl.when(me - d >= 0)
            def _():
                copy = a_copy(me - d, j, 0, d)
                copy.wait_recv()
                pl.when(to_right)(lambda: copy.start())

            @pl.when(me + d < n)
            def _():
                copy = a_copy(me + d, j, 1, d)
                copy.wait_recv()
                pl.when(to_left)(lambda: copy.start())

            after(d, j)

    pl.when(gap == n - 2)(finish)
    for j in range(chunks):
        after(n, j, last=True)
    pl.when(gap == n - 1)(finish)

    @pl.when(away)
    def _():
        @pl.loop(0, parts)
        def _(c):
            last_copy(c).wait()

    @pl.when(jnp.logical_not(away))
    def _():
        keep = pltpu.make_async_copy(final, o_ref, load_sems.at[0])
        keep.start()
        keep.wait()

    @pl.loop(0, n)
    def _(d):
        for way, fits, go in ((0, me - d >= 0, to_right), (1, me + d < n, to_left)):
            b = me - d if way == 0 else me + d

            @pl.when(jnp.logical_and(fits, go))
            def _():
                kv_copy(b, way, d).wait_send()
                for j in range(chunks):
                    a_copy(b, j, way, d).wait_send()

    @pl.loop(0, n // 2)
    def _(g):
        @pl.loop(0, parts)
        def _(c):
            core_copy(g, c).wait_send()
            pl.when(g != head)(lambda: head_copy(g, c).wait_send())


def on_device(queries, key_rows, value_rows, out_weight):
    tokens, width = queries.shape
    heads_here = width // HD
    group_ratio = QH // KVH
    pairs = max(heads_here // group_ratio, 1)
    per_pair = heads_here // pairs
    n = lax.axis_size("ctx")
    n_head = lax.axis_size("head")
    columns = out_weight.shape[1]
    block = (tokens, columns)
    groups = (n // 2,) + block
    chunks = min(CHUNKS, heads_here)
    parts = columns // TILE if columns % TILE == 0 else 1
    anywhere = pl.BlockSpec(memory_space=pl.ANY)
    dma = pltpu.SemaphoreType.DMA
    bf16 = jnp.bfloat16
    return pl.pallas_call(
        functools.partial(kernel, n, n_head, per_pair, pairs, chunks, parts),
        out_shape=jax.ShapeDtypeStruct(block, bf16),
        in_specs=[anywhere] * 4,
        out_specs=anywhere,
        scratch_shapes=[
            pltpu.VMEM((n * tokens, 2 * pairs * HD), bf16),
            pltpu.VMEM((pairs, n * tokens, 2 * HD), bf16),
            pltpu.VMEM((tokens, width), bf16),
            pltpu.VMEM((n, tokens, width), bf16),
            pltpu.VMEM(out_weight.shape, bf16),
            pltpu.VMEM(groups, bf16),
            pltpu.VMEM(groups, bf16),
            pltpu.VMEM(groups, bf16),
            pltpu.VMEM(groups, bf16),
            pltpu.VMEM((n_head,) + block, bf16),
            pltpu.VMEM(block, bf16),
            dma((4,)),
            dma((2, n)),
            dma((n,)),
            dma((2, n, chunks)),
            dma((n, chunks)),
            dma((n // 2, parts)),
            dma((n // 2, parts)),
            dma((n // 2, parts)),
            dma((n_head, parts)),
            dma((parts,)),
            dma((parts,)),
        ],
        compiler_params=pltpu.CompilerParams(
            collective_id=0, has_side_effects=True, vmem_limit_bytes=60 * 2**20
        ),
    )(key_rows, value_rows, queries, out_weight)


def solution(mesh):
    assert mesh.shape["sub"] == 2
    assert mesh.shape["ctx"] == mesh.shape["head"] * mesh.shape["sub"]
    return jax.shard_map(
        on_device,
        mesh=mesh,
        in_specs=(
            P(("groups", "ctx"), ("head", "sub")),
            P(("groups", "ctx"), "head"),
            P(("groups", "ctx"), "head"),
            P(("head", "sub"), "ctx"),
        ),
        out_specs=P(("groups", "ctx"), ("head", "sub")),
        check_vma=False,
    )
```

```python
import functools
import math

import jax
import jax.numpy as jnp
from jax import lax
from jax.experimental import pallas as pl
from jax.experimental.pallas import tpu as pltpu
from jax.sharding import PartitionSpec as P

QH = 64
KVH = 8
HD = 128
CHUNKS = 8
TILE = 256
ROWS = 128
MESH = pl.DeviceIdType.MESH


def kernel(
    n, n_head, per_pair, pairs, chunks, parts, k_hbm, v_hbm, q_hbm, w_hbm, o_ref,
    kv_all, v_ext, q_ref, att, w, own, out, rx1, summed, rx2, final,
    load_sems, kv_send, kv_recv, a_send, a_recv, s1, r1, s2, r2, s3, r3,
):
    me, head, sub = (lax.axis_index(a) for a in ("ctx", "head", "sub"))
    other = 1 - sub
    hs = head * 2 + sub
    tokens, width = q_ref.shape
    heads = width // HD
    columns = w.shape[1]
    piece = width // chunks
    to_right, to_left = me < n - 1, me > 0
    right, left = lax.min(me + 1, n - 1), lax.max(me - 1, 0)
    away = hs != me
    share = tokens // n_head

    def rows_of(b):
        return pl.ds(pl.multiple_of(b * tokens, tokens), tokens)

    first = pl.multiple_of((sub * heads // (QH // KVH)) * HD, HD)
    loads = [
        pltpu.make_async_copy(
            side.at[:, pl.ds(first, pairs * HD)],
            kv_all.at[rows_of(me), pl.ds(i * pairs * HD, pairs * HD)],
            load_sems.at[i],
        )
        for i, side in enumerate((k_hbm, v_hbm))
    ]
    loads.append(pltpu.make_async_copy(q_hbm, q_ref, load_sems.at[2]))
    loads.append(pltpu.make_async_copy(w_hbm, w, load_sems.at[3]))
    for load in loads:
        load.start()

    barrier = pltpu.get_barrier_semaphore()

    def greet(where):
        pl.semaphore_signal(barrier, inc=1, device_id=where, device_id_type=MESH)

    pl.when(to_right)(lambda: greet({"ctx": right}))
    pl.when(to_left)(lambda: greet({"ctx": left}))
    for h in range(n_head):
        source = {"ctx": hs, "head": h, "sub": me % 2}
        pl.when(jnp.logical_or(away, head != h))(functools.partial(greet, source))
    greet({"sub": other})
    for step in range(1, n_head):
        greet({"head": lax.rem(head + step, n_head)})
    count = 2 * n_head - 1 + to_right.astype(jnp.int32) + to_left.astype(jnp.int32)
    pl.semaphore_wait(barrier, count + away.astype(jnp.int32))

    def remote(src, dst, send, recv, where):
        return pltpu.make_async_remote_copy(
            src_ref=src, dst_ref=dst, send_sem=send, recv_sem=recv, device_id=where, device_id_type=MESH
        )

    def kv_copy(b, way, d):
        where = {"ctx": right if way == 0 else left}
        part = kv_all.at[rows_of(b)]
        return remote(part, part, kv_send.at[way, d], kv_recv.at[b], where)

    loads[0].wait()
    loads[1].wait()
    pl.when(to_right)(lambda: kv_copy(me, 0, 0).start())
    pl.when(to_left)(lambda: kv_copy(me, 1, 0).start())

    @pl.loop(1, n)
    def _(d):
        @pl.when(me - d >= 0)
        def _():
            copy = kv_copy(me - d, 0, d)
            copy.wait_recv()
            pl.when(to_right)(lambda: copy.start())

        @pl.when(me + d < n)
        def _():
            copy = kv_copy(me + d, 1, d)
            copy.wait_recv()
            pl.when(to_left)(lambda: copy.start())

    loads[2].wait()

    def a_copy(b, j, way, d):
        where = {"ctx": right if way == 0 else left}
        part = att.at[b, :, pl.ds(j * piece, piece)]
        return remote(part, part, a_send.at[way, d, j], a_recv.at[b, j], where)

    factor = math.log2(math.e) / HD**0.5
    for j in range(chunks):
        if j % (chunks // pairs) == 0:
            p = j // (chunks // pairs)
            v_ext[p, :, :HD] = kv_all[:, (pairs + p) * HD : (pairs + p + 1) * HD]
            v_ext[p, :, HD:] = jnp.ones((v_ext.shape[1], HD), v_ext.dtype)

        @pl.loop(j * heads // chunks, (j + 1) * heads // chunks)
        def _(h):
            pair = h // per_pair
            cols = pl.ds(pl.multiple_of(h * HD, HD), HD)
            keys = kv_all[:, pl.ds(pl.multiple_of(pair * HD, HD), HD)]
            for start in range(0, tokens, ROWS):
                rows = pl.ds(start, ROWS)
                scores = lax.dot_general(
                    q_ref[rows, cols], keys, (((1,), (1,)), ((), ())), preferred_element_type=jnp.float32
                )
                row_max = jnp.max(scores, axis=1, keepdims=True)
                weights = jnp.exp2((scores - row_max) * factor).astype(jnp.bfloat16)
                both = jnp.dot(weights, v_ext[pair], preferred_element_type=jnp.float32)
                att[me, rows, cols] = (both[:, :HD] / both[:, HD:]).astype(att.dtype)

        pl.when(to_right)(lambda: a_copy(me, j, 0, 0).start())
        pl.when(to_left)(lambda: a_copy(me, j, 1, 0).start())

    loads[3].wait()
    tile = columns // parts

    def cols_of(c):
        return pl.ds(0, columns) if parts == 1 else pl.ds(pl.multiple_of(c * tile, tile), tile)

    def core_copy(g, c):
        cols = cols_of(c)
        return remote(out.at[g, :, cols], rx1.at[g, :, cols], s1.at[g, c], r1.at[g, c], {"sub": other})

    def share_of(h):
        return pl.ds(pl.multiple_of(h * share, share), share)

    def head_copy(g, step, c):
        cols, target = cols_of(c), lax.rem(head + step, n_head)
        return remote(
            summed.at[g, share_of(target), cols], rx2.at[g, head, :, cols],
            s2.at[g, step - 1, c], r2.at[g, head, c], {"head": target},
        )

    def head_arrival(g, source, c):
        cols = cols_of(c)
        return remote(
            summed.at[g, share_of(source), cols], rx2.at[g, source, :, cols],
            s2.at[g, 0, c], r2.at[g, source, c], {"head": source},
        )

    def last_copy(g, h, c):
        cols = cols_of(c)
        where = {"ctx": 2 * g + sub, "head": me // 2, "sub": me % 2}
        return remote(final.at[g, :, cols], o_ref.at[share_of(h), cols], s3.at[g, c], r3.at[h, c], where)

    def product(t, c):
        cols = cols_of(c)
        return jnp.dot(att[t], w[:, cols], preferred_element_type=jnp.float32).astype(out.dtype)

    def multiply(t):
        g = t // 2

        @pl.when(t % 2 == sub)
        def _():
            @pl.loop(0, parts)
            def _(c):
                own[g, :, cols_of(c)] = product(t, c)

        @pl.when(t % 2 != sub)
        def _():
            @pl.loop(0, parts)
            def _(c):
                out[g, :, cols_of(c)] = product(t, c)
                core_copy(g, c).start()

    def combine(t):
        g = t // 2

        @pl.when(t % 2 == sub)
        def _():
            @pl.loop(0, parts)
            def _(c):
                cols = cols_of(c)
                core_copy(g, c).wait_recv()
                total = own[g, :, cols].astype(jnp.float32) + rx1[g, :, cols].astype(jnp.float32)
                summed[g, :, cols] = total.astype(summed.dtype)
                for step in range(1, n_head):
                    head_copy(g, step, c).start()

    def finish(t):
        g = t // 2

        @pl.when(t % 2 == sub)
        def _():
            @pl.loop(0, parts)
            def _(c):
                cols = cols_of(c)
                total = summed[g, share_of(head), cols].astype(jnp.float32)
                for step in range(1, n_head):
                    source = lax.rem(head + step, n_head)
                    head_arrival(g, source, c).wait_recv()
                    total += rx2[g, source, :, cols].astype(jnp.float32)
                final[g, :, cols] = total.astype(final.dtype)
                pl.when(jnp.logical_or(away, t != me))(lambda: last_copy(g, head, c).start())

    def finish_at(d):
        pl.when(jnp.logical_and(d >= 0, me - d >= 0))(lambda: finish(me - d))
        pl.when(jnp.logical_and(d > 0, me + d < n))(lambda: finish(me + d))

    def after(d, j, last=False):
        behind, ahead = me - d + 1, me + d - 1
        if j == 0:
            pl.when(behind >= 0)(lambda: multiply(behind))
        if j == chunks // 4:
            pl.when(jnp.logical_and(ahead < n, d > 1))(lambda: multiply(ahead))
        if j == chunks // 2:
            pl.when(behind >= 0)(lambda: combine(behind))
        if j == chunks // 2 + 1:
            pl.when(jnp.logical_and(ahead < n, d > 1))(lambda: combine(ahead))
        if j == chunks - 1 and not last:
            finish_at(d - 2)

    @pl.loop(1, n)
    def _(d):
        for j in range(chunks):

            @pl.when(me - d >= 0)
            def _():
                copy = a_copy(me - d, j, 0, d)
                copy.wait_recv()
                pl.when(to_right)(lambda: copy.start())

            @pl.when(me + d < n)
            def _():
                copy = a_copy(me + d, j, 1, d)
                copy.wait_recv()
                pl.when(to_left)(lambda: copy.start())

            after(d, j)

    finish_at(n - 2)
    for j in range(chunks):
        after(n, j, last=True)
    finish_at(n - 1)

    @pl.when(jnp.logical_not(away))
    def _():
        keep = pltpu.make_async_copy(final.at[me // 2], o_ref.at[share_of(head)], load_sems.at[0])
        keep.start()
        keep.wait()

    for h in range(n_head):

        @pl.when(jnp.logical_or(away, head != h))
        def _():
            @pl.loop(0, parts)
            def _(c):
                last_copy(0, h, c).wait_recv()

    @pl.loop(0, n)
    def _(d):
        for way, fits, go in ((0, me - d >= 0, to_right), (1, me + d < n, to_left)):
            b = me - d if way == 0 else me + d

            @pl.when(jnp.logical_and(fits, go))
            def _():
                kv_copy(b, way, d).wait_send()
                for j in range(chunks):
                    a_copy(b, j, way, d).wait_send()

    @pl.loop(0, n // 2)
    def _(g):
        @pl.loop(0, parts)
        def _(c):
            core_copy(g, c).wait_send()
            for step in range(1, n_head):
                head_copy(g, step, c).wait_send()
            pl.when(jnp.logical_or(away, 2 * g + sub != me))(lambda: last_copy(g, head, c).wait_send())


def on_device(queries, key_rows, value_rows, out_weight):
    tokens, width = queries.shape
    heads_here = width // HD
    group_ratio = QH // KVH
    pairs = max(heads_here // group_ratio, 1)
    per_pair = heads_here // pairs
    n = lax.axis_size("ctx")
    n_head = lax.axis_size("head")
    columns = out_weight.shape[1]
    block = (tokens, columns)
    groups = (n // 2,) + block
    chunks = min(CHUNKS, heads_here)
    parts = columns // TILE if columns % TILE == 0 else 1
    anywhere = pl.BlockSpec(memory_space=pl.ANY)
    dma = pltpu.SemaphoreType.DMA
    bf16 = jnp.bfloat16
    return pl.pallas_call(
        functools.partial(kernel, n, n_head, per_pair, pairs, chunks, parts),
        out_shape=jax.ShapeDtypeStruct(block, bf16),
        in_specs=[anywhere] * 4,
        out_specs=anywhere,
        scratch_shapes=[
            pltpu.VMEM((n * tokens, 2 * pairs * HD), bf16),
            pltpu.VMEM((pairs, n * tokens, 2 * HD), bf16),
            pltpu.VMEM((tokens, width), bf16),
            pltpu.VMEM((n, tokens, width), bf16),
            pltpu.VMEM(out_weight.shape, bf16),
            pltpu.VMEM(groups, bf16),
            pltpu.VMEM(groups, bf16),
            pltpu.VMEM(groups, bf16),
            pltpu.VMEM(groups, bf16),
            pltpu.VMEM((n // 2, n_head, tokens // n_head, columns), bf16),
            pltpu.VMEM((n // 2, tokens // n_head, columns), bf16),
            dma((4,)),
            dma((2, n)),
            dma((n,)),
            dma((2, n, chunks)),
            dma((n, chunks)),
            dma((n // 2, parts)),
            dma((n // 2, parts)),
            dma((n // 2, n_head - 1, parts)),
            dma((n // 2, n_head, parts)),
            dma((n // 2, parts)),
            dma((n_head, parts)),
        ],
        compiler_params=pltpu.CompilerParams(
            collective_id=0, has_side_effects=True, vmem_limit_bytes=60 * 2**20
        ),
    )(key_rows, value_rows, queries, out_weight)


def solution(mesh):
    assert mesh.shape["sub"] == 2
    assert mesh.shape["ctx"] == mesh.shape["head"] * mesh.shape["sub"]
    return jax.shard_map(
        on_device,
        mesh=mesh,
        in_specs=(
            P(("groups", "ctx"), ("head", "sub")),
            P(("groups", "ctx"), "head"),
            P(("groups", "ctx"), "head"),
            P(("head", "sub"), "ctx"),
        ),
        out_specs=P(("groups", "ctx"), ("head", "sub")),
        check_vma=False,
    )
```

```python
import functools
import math

import jax
import jax.numpy as jnp
from jax import lax
from jax.experimental import pallas as pl
from jax.experimental.pallas import tpu as pltpu
from jax.sharding import PartitionSpec as P

QH = 64
KVH = 8
HD = 128
CHUNKS = 8
TILE = 256
ROWS = 128
MESH = pl.DeviceIdType.MESH


def kernel(
    n, n_head, per_pair, pairs, chunks, parts, k_hbm, v_hbm, q_hbm, w_hbm, o_ref,
    kv_all, v_ext, q_ref, att, w, own, out, rx1, summed, rx2, final,
    load_sems, kv_send, kv_recv, a_send, a_recv, s1, r1, s2, r2, s3, r3,
):
    me, head, sub = (lax.axis_index(a) for a in ("ctx", "head", "sub"))
    other = 1 - sub
    hs = head * 2 + sub
    tokens, width = q_ref.shape
    heads = width // HD
    columns = w.shape[1]
    piece = width // chunks
    to_right, to_left = me < n - 1, me > 0
    right, left = lax.min(me + 1, n - 1), lax.max(me - 1, 0)
    away = hs != me
    share = tokens // n_head

    def rows_of(b):
        return pl.ds(pl.multiple_of(b * tokens, tokens), tokens)

    first = pl.multiple_of((sub * heads // (QH // KVH)) * HD, HD)
    loads = [
        pltpu.make_async_copy(
            side.at[:, pl.ds(first, pairs * HD)],
            kv_all.at[rows_of(me), pl.ds(i * pairs * HD, pairs * HD)],
            load_sems.at[i],
        )
        for i, side in enumerate((k_hbm, v_hbm))
    ]
    loads.append(pltpu.make_async_copy(q_hbm, q_ref, load_sems.at[2]))
    loads.append(pltpu.make_async_copy(w_hbm, w, load_sems.at[3]))
    for load in loads:
        load.start()

    barrier = pltpu.get_barrier_semaphore()

    def greet(where):
        pl.semaphore_signal(barrier, inc=1, device_id=where, device_id_type=MESH)

    pl.when(to_right)(lambda: greet({"ctx": right}))
    pl.when(to_left)(lambda: greet({"ctx": left}))
    for h in range(n_head):
        source = {"ctx": hs, "head": h, "sub": me % 2}
        pl.when(jnp.logical_or(away, head != h))(functools.partial(greet, source))
    greet({"sub": other})
    for step in range(1, n_head):
        greet({"head": lax.rem(head + step, n_head)})
    count = 2 * n_head - 1 + to_right.astype(jnp.int32) + to_left.astype(jnp.int32)
    pl.semaphore_wait(barrier, count + away.astype(jnp.int32))

    def remote(src, dst, send, recv, where):
        return pltpu.make_async_remote_copy(
            src_ref=src, dst_ref=dst, send_sem=send, recv_sem=recv, device_id=where, device_id_type=MESH
        )

    def kv_copy(b, way, d):
        where = {"ctx": right if way == 0 else left}
        part = kv_all.at[rows_of(b)]
        return remote(part, part, kv_send.at[way, d], kv_recv.at[b], where)

    loads[0].wait()
    loads[1].wait()
    pl.when(to_right)(lambda: kv_copy(me, 0, 0).start())
    pl.when(to_left)(lambda: kv_copy(me, 1, 0).start())

    @pl.loop(1, n)
    def _(d):
        @pl.when(me - d >= 0)
        def _():
            copy = kv_copy(me - d, 0, d)
            copy.wait_recv()
            pl.when(to_right)(lambda: copy.start())

        @pl.when(me + d < n)
        def _():
            copy = kv_copy(me + d, 1, d)
            copy.wait_recv()
            pl.when(to_left)(lambda: copy.start())

    loads[2].wait()

    def a_copy(b, j, way, d):
        where = {"ctx": right if way == 0 else left}
        part = att.at[b, :, pl.ds(j * piece, piece)]
        return remote(part, part, a_send.at[way, d, j], a_recv.at[b, j], where)

    factor = math.log2(math.e) / HD**0.5
    for j in range(chunks):
        if j % (chunks // pairs) == 0:
            p = j // (chunks // pairs)
            v_ext[p, :, :HD] = kv_all[:, (pairs + p) * HD : (pairs + p + 1) * HD]
            v_ext[p, :, HD:] = jnp.ones((v_ext.shape[1], HD), v_ext.dtype)

        @pl.loop(j * heads // chunks, (j + 1) * heads // chunks)
        def _(h):
            pair = h // per_pair
            cols = pl.ds(pl.multiple_of(h * HD, HD), HD)
            keys = kv_all[:, pl.ds(pl.multiple_of(pair * HD, HD), HD)]
            for start in range(0, tokens, ROWS):
                rows = pl.ds(start, ROWS)
                scores = lax.dot_general(
                    q_ref[rows, cols], keys, (((1,), (1,)), ((), ())), preferred_element_type=jnp.float32
                )
                row_max = jnp.max(scores, axis=1, keepdims=True)
                weights = jnp.exp2((scores - row_max) * factor).astype(jnp.bfloat16)
                both = jnp.dot(weights, v_ext[pair], preferred_element_type=jnp.float32)
                att[me, rows, cols] = (both[:, :HD] / both[:, HD:]).astype(att.dtype)

        pl.when(to_right)(lambda: a_copy(me, j, 0, 0).start())
        pl.when(to_left)(lambda: a_copy(me, j, 1, 0).start())

    loads[3].wait()
    tile = columns // parts

    def cols_of(c):
        return pl.ds(0, columns) if parts == 1 else pl.ds(pl.multiple_of(c * tile, tile), tile)

    def core_copy(g, c):
        cols = cols_of(c)
        return remote(out.at[g, :, cols], rx1.at[g, :, cols], s1.at[g, c], r1.at[g, c], {"sub": other})

    def share_of(h):
        return pl.ds(pl.multiple_of(h * share, share), share)

    def head_copy(g, step, c):
        cols, target = cols_of(c), lax.rem(head + step, n_head)
        return remote(
            summed.at[g, share_of(target), cols], rx2.at[g, head, :, cols],
            s2.at[g, step - 1, c], r2.at[g, head, c], {"head": target},
        )

    def head_arrival(g, source, c):
        cols = cols_of(c)
        return remote(
            summed.at[g, share_of(source), cols], rx2.at[g, source, :, cols],
            s2.at[g, 0, c], r2.at[g, source, c], {"head": source},
        )

    def last_copy(g, h, c):
        cols = cols_of(c)
        where = {"ctx": 2 * g + sub, "head": me // 2, "sub": me % 2}
        return remote(final.at[g, :, cols], o_ref.at[share_of(h), cols], s3.at[g, c], r3.at[h, c], where)

    def product(t, c):
        cols = cols_of(c)
        return jnp.dot(att[t], w[:, cols], preferred_element_type=jnp.float32).astype(out.dtype)

    def multiply(t):
        g = t // 2

        @pl.when(t % 2 == sub)
        def _():
            @pl.loop(0, parts)
            def _(c):
                own[g, :, cols_of(c)] = product(t, c)

        @pl.when(t % 2 != sub)
        def _():
            @pl.loop(0, parts)
            def _(c):
                out[g, :, cols_of(c)] = product(t, c)
                core_copy(g, c).start()

    def combine(t):
        g = t // 2

        @pl.when(t % 2 == sub)
        def _():
            @pl.loop(0, parts)
            def _(c):
                cols = cols_of(c)
                core_copy(g, c).wait_recv()
                total = own[g, :, cols].astype(jnp.float32) + rx1[g, :, cols].astype(jnp.float32)
                summed[g, :, cols] = total.astype(summed.dtype)
                for step in range(1, n_head):
                    head_copy(g, step, c).start()

    def finish(t):
        g = t // 2

        @pl.when(t % 2 == sub)
        def _():
            @pl.loop(0, parts)
            def _(c):
                cols = cols_of(c)
                total = summed[g, share_of(head), cols].astype(jnp.float32)
                for step in range(1, n_head):
                    source = lax.rem(head + step, n_head)
                    head_arrival(g, source, c).wait_recv()
                    total += rx2[g, source, :, cols].astype(jnp.float32)
                final[g, :, cols] = total.astype(final.dtype)
                pl.when(jnp.logical_or(away, t != me))(lambda: last_copy(g, head, c).start())

    def finish_at(d, late):
        for t, fits in ((me - d, d >= 0), (me + d, d > 0)):
            at_end = jnp.logical_and(jnp.logical_or(t == 0, t == n - 1), t != me)
            now = at_end if late else jnp.logical_not(at_end)
            inside = jnp.logical_and(t >= 0, t < n)
            pl.when(jnp.logical_and(jnp.logical_and(fits, inside), now))(functools.partial(finish, t))

    def after(d, j, last=False):
        behind, ahead = me - d + 1, me + d - 1
        if j == 0:
            pl.when(behind >= 0)(lambda: multiply(behind))
        if j == chunks // 4:
            pl.when(jnp.logical_and(ahead < n, d > 1))(lambda: multiply(ahead))
        if j == chunks // 2:
            pl.when(behind >= 0)(lambda: combine(behind))
        if j == chunks // 2 + 1:
            pl.when(jnp.logical_and(ahead < n, d > 1))(lambda: combine(ahead))
        if j == chunks - 1 and not last:
            finish_at(d - 2, False)

    @pl.loop(1, n)
    def _(d):
        for j in range(chunks):

            @pl.when(me - d >= 0)
            def _():
                copy = a_copy(me - d, j, 0, d)
                copy.wait_recv()
                pl.when(to_right)(lambda: copy.start())

            @pl.when(me + d < n)
            def _():
                copy = a_copy(me + d, j, 1, d)
                copy.wait_recv()
                pl.when(to_left)(lambda: copy.start())

            after(d, j)

    finish_at(n - 2, False)

    @pl.loop(1, n - 1)
    def _(d):
        finish_at(d, True)

    for j in range(chunks):
        after(n, j, last=True)
    finish_at(n - 1, True)

    @pl.when(jnp.logical_not(away))
    def _():
        keep = pltpu.make_async_copy(final.at[me // 2], o_ref.at[share_of(head)], load_sems.at[0])
        keep.start()
        keep.wait()

    for h in range(n_head):

        @pl.when(jnp.logical_or(away, head != h))
        def _():
            @pl.loop(0, parts)
            def _(c):
                last_copy(0, h, c).wait_recv()

    @pl.loop(0, n)
    def _(d):
        for way, fits, go in ((0, me - d >= 0, to_right), (1, me + d < n, to_left)):
            b = me - d if way == 0 else me + d

            @pl.when(jnp.logical_and(fits, go))
            def _():
                kv_copy(b, way, d).wait_send()
                for j in range(chunks):
                    a_copy(b, j, way, d).wait_send()

    @pl.loop(0, n // 2)
    def _(g):
        @pl.loop(0, parts)
        def _(c):
            core_copy(g, c).wait_send()
            for step in range(1, n_head):
                head_copy(g, step, c).wait_send()
            pl.when(jnp.logical_or(away, 2 * g + sub != me))(lambda: last_copy(g, head, c).wait_send())


def on_device(queries, key_rows, value_rows, out_weight):
    tokens, width = queries.shape
    heads_here = width // HD
    group_ratio = QH // KVH
    pairs = max(heads_here // group_ratio, 1)
    per_pair = heads_here // pairs
    n = lax.axis_size("ctx")
    n_head = lax.axis_size("head")
    columns = out_weight.shape[1]
    block = (tokens, columns)
    groups = (n // 2,) + block
    chunks = min(CHUNKS, heads_here)
    parts = columns // TILE if columns % TILE == 0 else 1
    anywhere = pl.BlockSpec(memory_space=pl.ANY)
    dma = pltpu.SemaphoreType.DMA
    bf16 = jnp.bfloat16
    return pl.pallas_call(
        functools.partial(kernel, n, n_head, per_pair, pairs, chunks, parts),
        out_shape=jax.ShapeDtypeStruct(block, bf16),
        in_specs=[anywhere] * 4,
        out_specs=anywhere,
        scratch_shapes=[
            pltpu.VMEM((n * tokens, 2 * pairs * HD), bf16),
            pltpu.VMEM((pairs, n * tokens, 2 * HD), bf16),
            pltpu.VMEM((tokens, width), bf16),
            pltpu.VMEM((n, tokens, width), bf16),
            pltpu.VMEM(out_weight.shape, bf16),
            pltpu.VMEM(groups, bf16),
            pltpu.VMEM(groups, bf16),
            pltpu.VMEM(groups, bf16),
            pltpu.VMEM(groups, bf16),
            pltpu.VMEM((n // 2, n_head, tokens // n_head, columns), bf16),
            pltpu.VMEM((n // 2, tokens // n_head, columns), bf16),
            dma((4,)),
            dma((2, n)),
            dma((n,)),
            dma((2, n, chunks)),
            dma((n, chunks)),
            dma((n // 2, parts)),
            dma((n // 2, parts)),
            dma((n // 2, n_head - 1, parts)),
            dma((n // 2, n_head, parts)),
            dma((n // 2, parts)),
            dma((n_head, parts)),
        ],
        compiler_params=pltpu.CompilerParams(
            collective_id=0, has_side_effects=True, vmem_limit_bytes=60 * 2**20
        ),
    )(key_rows, value_rows, queries, out_weight)


def solution(mesh):
    assert mesh.shape["sub"] == 2
    assert mesh.shape["ctx"] == mesh.shape["head"] * mesh.shape["sub"]
    return jax.shard_map(
        on_device,
        mesh=mesh,
        in_specs=(
            P(("groups", "ctx"), ("head", "sub")),
            P(("groups", "ctx"), "head"),
            P(("groups", "ctx"), "head"),
            P(("head", "sub"), "ctx"),
        ),
        out_specs=P(("groups", "ctx"), ("head", "sub")),
        check_vma=False,
    )
```

```python
import functools
import math

import jax
import jax.numpy as jnp
from jax import lax
from jax.experimental import pallas as pl
from jax.experimental.pallas import tpu as pltpu
from jax.sharding import PartitionSpec as P

QH = 64
KVH = 8
HD = 128
CHUNKS = 16
TILE = 256
ROWS = 128
MESH = pl.DeviceIdType.MESH


def kernel(
    n, n_head, per_pair, pairs, chunks, parts, k_hbm, v_hbm, q_hbm, w_hbm, o_ref,
    kv_all, v_ext, q_ref, att, w, own, out, rx1, summed, rx2, final,
    load_sems, kv_send, kv_recv, a_send, a_recv, s1, r1, s2, r2, s3, r3,
):
    me, head, sub = (lax.axis_index(a) for a in ("ctx", "head", "sub"))
    other = 1 - sub
    hs = head * 2 + sub
    tokens, width = q_ref.shape
    heads = width // HD
    columns = w.shape[1]
    piece = width // chunks
    to_right, to_left = me < n - 1, me > 0
    right, left = lax.min(me + 1, n - 1), lax.max(me - 1, 0)
    away = hs != me
    share = tokens // n_head

    def rows_of(b):
        return pl.ds(pl.multiple_of(b * tokens, tokens), tokens)

    first = pl.multiple_of((sub * heads // (QH // KVH)) * HD, HD)
    loads = [
        pltpu.make_async_copy(
            side.at[:, pl.ds(first, pairs * HD)],
            kv_all.at[rows_of(me), pl.ds(i * pairs * HD, pairs * HD)],
            load_sems.at[i],
        )
        for i, side in enumerate((k_hbm, v_hbm))
    ]
    loads.append(pltpu.make_async_copy(q_hbm, q_ref, load_sems.at[2]))
    loads.append(pltpu.make_async_copy(w_hbm, w, load_sems.at[3]))
    for load in loads:
        load.start()

    barrier = pltpu.get_barrier_semaphore()

    def greet(where):
        pl.semaphore_signal(barrier, inc=1, device_id=where, device_id_type=MESH)

    pl.when(to_right)(lambda: greet({"ctx": right}))
    pl.when(to_left)(lambda: greet({"ctx": left}))
    for h in range(n_head):
        source = {"ctx": hs, "head": h, "sub": me % 2}
        pl.when(jnp.logical_or(away, head != h))(functools.partial(greet, source))
    greet({"sub": other})
    for step in range(1, n_head):
        greet({"head": lax.rem(head + step, n_head)})
    count = 2 * n_head - 1 + to_right.astype(jnp.int32) + to_left.astype(jnp.int32)
    pl.semaphore_wait(barrier, count + away.astype(jnp.int32))

    def remote(src, dst, send, recv, where):
        return pltpu.make_async_remote_copy(
            src_ref=src, dst_ref=dst, send_sem=send, recv_sem=recv, device_id=where, device_id_type=MESH
        )

    def kv_copy(b, way, d):
        where = {"ctx": right if way == 0 else left}
        part = kv_all.at[rows_of(b)]
        return remote(part, part, kv_send.at[way, d], kv_recv.at[b], where)

    loads[0].wait()
    loads[1].wait()
    pl.when(to_right)(lambda: kv_copy(me, 0, 0).start())
    pl.when(to_left)(lambda: kv_copy(me, 1, 0).start())

    @pl.loop(1, n)
    def _(d):
        @pl.when(me - d >= 0)
        def _():
            copy = kv_copy(me - d, 0, d)
            copy.wait_recv()
            pl.when(to_right)(lambda: copy.start())

        @pl.when(me + d < n)
        def _():
            copy = kv_copy(me + d, 1, d)
            copy.wait_recv()
            pl.when(to_left)(lambda: copy.start())

    loads[2].wait()

    def a_copy(b, j, way, d):
        where = {"ctx": right if way == 0 else left}
        part = att.at[b, :, pl.ds(j * piece, piece)]
        return remote(part, part, a_send.at[way, d, j], a_recv.at[b, j], where)

    factor = math.log2(math.e) / HD**0.5
    for j in range(chunks):
        if j % (chunks // pairs) == 0:
            p = j // (chunks // pairs)
            v_ext[p, :, :HD] = kv_all[:, (pairs + p) * HD : (pairs + p + 1) * HD]
            v_ext[p, :, HD:] = jnp.ones((v_ext.shape[1], HD), v_ext.dtype)

        @pl.loop(j * heads // chunks, (j + 1) * heads // chunks)
        def _(h):
            pair = h // per_pair
            cols = pl.ds(pl.multiple_of(h * HD, HD), HD)
            keys = kv_all[:, pl.ds(pl.multiple_of(pair * HD, HD), HD)]
            for start in range(0, tokens, ROWS):
                rows = pl.ds(start, ROWS)
                scores = lax.dot_general(
                    q_ref[rows, cols], keys, (((1,), (1,)), ((), ())), preferred_element_type=jnp.float32
                )
                row_max = jnp.max(scores, axis=1, keepdims=True)
                weights = jnp.exp2((scores - row_max) * factor).astype(jnp.bfloat16)
                both = jnp.dot(weights, v_ext[pair], preferred_element_type=jnp.float32)
                att[me, rows, cols] = (both[:, :HD] / both[:, HD:]).astype(att.dtype)

        pl.when(to_right)(lambda: a_copy(me, j, 0, 0).start())
        pl.when(to_left)(lambda: a_copy(me, j, 1, 0).start())

    loads[3].wait()
    tile = columns // parts

    def cols_of(c):
        return pl.ds(0, columns) if parts == 1 else pl.ds(pl.multiple_of(c * tile, tile), tile)

    def core_copy(g, c):
        cols = cols_of(c)
        return remote(out.at[g, :, cols], rx1.at[g, :, cols], s1.at[g, c], r1.at[g, c], {"sub": other})

    def share_of(h):
        return pl.ds(pl.multiple_of(h * share, share), share)

    def head_copy(g, step, c):
        cols, target = cols_of(c), lax.rem(head + step, n_head)
        return remote(
            summed.at[g, share_of(target), cols], rx2.at[g, head, :, cols],
            s2.at[g, step - 1, c], r2.at[g, head, c], {"head": target},
        )

    def head_arrival(g, source, c):
        cols = cols_of(c)
        return remote(
            summed.at[g, share_of(source), cols], rx2.at[g, source, :, cols],
            s2.at[g, 0, c], r2.at[g, source, c], {"head": source},
        )

    def last_copy(g, h, c):
        cols = cols_of(c)
        where = {"ctx": 2 * g + sub, "head": me // 2, "sub": me % 2}
        return remote(final.at[g, :, cols], o_ref.at[share_of(h), cols], s3.at[g, c], r3.at[h, c], where)

    def product(t, c):
        cols = cols_of(c)
        return jnp.dot(att[t], w[:, cols], preferred_element_type=jnp.float32).astype(out.dtype)

    def multiply(t):
        g = t // 2

        @pl.when(t % 2 == sub)
        def _():
            @pl.loop(0, parts)
            def _(c):
                own[g, :, cols_of(c)] = product(t, c)

        @pl.when(t % 2 != sub)
        def _():
            @pl.loop(0, parts)
            def _(c):
                out[g, :, cols_of(c)] = product(t, c)
                core_copy(g, c).start()

    def combine(t):
        g = t // 2

        @pl.when(t % 2 == sub)
        def _():
            @pl.loop(0, parts)
            def _(c):
                cols = cols_of(c)
                core_copy(g, c).wait_recv()
                total = own[g, :, cols].astype(jnp.float32) + rx1[g, :, cols].astype(jnp.float32)
                summed[g, :, cols] = total.astype(summed.dtype)
                for step in range(1, n_head):
                    head_copy(g, step, c).start()

    def finish(t):
        g = t // 2

        @pl.when(t % 2 == sub)
        def _():
            @pl.loop(0, parts)
            def _(c):
                cols = cols_of(c)
                total = summed[g, share_of(head), cols].astype(jnp.float32)
                for step in range(1, n_head):
                    source = lax.rem(head + step, n_head)
                    head_arrival(g, source, c).wait_recv()
                    total += rx2[g, source, :, cols].astype(jnp.float32)
                final[g, :, cols] = total.astype(final.dtype)
                pl.when(jnp.logical_or(away, t != me))(lambda: last_copy(g, head, c).start())

    def finish_at(d):
        pl.when(jnp.logical_and(d >= 0, me - d >= 0))(lambda: finish(me - d))
        pl.when(jnp.logical_and(d > 0, me + d < n))(lambda: finish(me + d))

    def after(d, j, last=False):
        behind, ahead = me - d + 1, me + d - 1
        if j == 0:
            pl.when(behind >= 0)(lambda: multiply(behind))
        if j == chunks // 4:
            pl.when(jnp.logical_and(ahead < n, d > 1))(lambda: multiply(ahead))
        if j == chunks // 2:
            pl.when(behind >= 0)(lambda: combine(behind))
        if j == chunks // 2 + 1:
            pl.when(jnp.logical_and(ahead < n, d > 1))(lambda: combine(ahead))
        if j == chunks - 1 and not last:
            finish_at(d - 2)

    @pl.loop(1, n)
    def _(d):
        for j in range(chunks):

            @pl.when(me - d >= 0)
            def _():
                copy = a_copy(me - d, j, 0, d)
                copy.wait_recv()
                pl.when(to_right)(lambda: copy.start())

            @pl.when(me + d < n)
            def _():
                copy = a_copy(me + d, j, 1, d)
                copy.wait_recv()
                pl.when(to_left)(lambda: copy.start())

            after(d, j)

    finish_at(n - 2)
    for j in range(chunks):
        after(n, j, last=True)
    finish_at(n - 1)

    @pl.when(jnp.logical_not(away))
    def _():
        keep = pltpu.make_async_copy(final.at[me // 2], o_ref.at[share_of(head)], load_sems.at[0])
        keep.start()
        keep.wait()

    for h in range(n_head):

        @pl.when(jnp.logical_or(away, head != h))
        def _():
            @pl.loop(0, parts)
            def _(c):
                last_copy(0, h, c).wait_recv()

    @pl.loop(0, n)
    def _(d):
        for way, fits, go in ((0, me - d >= 0, to_right), (1, me + d < n, to_left)):
            b = me - d if way == 0 else me + d

            @pl.when(jnp.logical_and(fits, go))
            def _():
                kv_copy(b, way, d).wait_send()
                for j in range(chunks):
                    a_copy(b, j, way, d).wait_send()

    @pl.loop(0, n // 2)
    def _(g):
        @pl.loop(0, parts)
        def _(c):
            core_copy(g, c).wait_send()
            for step in range(1, n_head):
                head_copy(g, step, c).wait_send()
            pl.when(jnp.logical_or(away, 2 * g + sub != me))(lambda: last_copy(g, head, c).wait_send())


def on_device(queries, key_rows, value_rows, out_weight):
    tokens, width = queries.shape
    heads_here = width // HD
    group_ratio = QH // KVH
    pairs = max(heads_here // group_ratio, 1)
    per_pair = heads_here // pairs
    n = lax.axis_size("ctx")
    n_head = lax.axis_size("head")
    columns = out_weight.shape[1]
    block = (tokens, columns)
    groups = (n // 2,) + block
    chunks = min(CHUNKS, heads_here)
    parts = columns // TILE if columns % TILE == 0 else 1
    anywhere = pl.BlockSpec(memory_space=pl.ANY)
    dma = pltpu.SemaphoreType.DMA
    bf16 = jnp.bfloat16
    return pl.pallas_call(
        functools.partial(kernel, n, n_head, per_pair, pairs, chunks, parts),
        out_shape=jax.ShapeDtypeStruct(block, bf16),
        in_specs=[anywhere] * 4,
        out_specs=anywhere,
        scratch_shapes=[
            pltpu.VMEM((n * tokens, 2 * pairs * HD), bf16),
            pltpu.VMEM((pairs, n * tokens, 2 * HD), bf16),
            pltpu.VMEM((tokens, width), bf16),
            pltpu.VMEM((n, tokens, width), bf16),
            pltpu.VMEM(out_weight.shape, bf16),
            pltpu.VMEM(groups, bf16),
            pltpu.VMEM(groups, bf16),
            pltpu.VMEM(groups, bf16),
            pltpu.VMEM(groups, bf16),
            pltpu.VMEM((n // 2, n_head, tokens // n_head, columns), bf16),
            pltpu.VMEM((n // 2, tokens // n_head, columns), bf16),
            dma((4,)),
            dma((2, n)),
            dma((n,)),
            dma((2, n, chunks)),
            dma((n, chunks)),
            dma((n // 2, parts)),
            dma((n // 2, parts)),
            dma((n // 2, n_head - 1, parts)),
            dma((n // 2, n_head, parts)),
            dma((n // 2, parts)),
            dma((n_head, parts)),
        ],
        compiler_params=pltpu.CompilerParams(
            collective_id=0, has_side_effects=True, vmem_limit_bytes=60 * 2**20
        ),
    )(key_rows, value_rows, queries, out_weight)


def solution(mesh):
    assert mesh.shape["sub"] == 2
    assert mesh.shape["ctx"] == mesh.shape["head"] * mesh.shape["sub"]
    return jax.shard_map(
        on_device,
        mesh=mesh,
        in_specs=(
            P(("groups", "ctx"), ("head", "sub")),
            P(("groups", "ctx"), "head"),
            P(("groups", "ctx"), "head"),
            P(("head", "sub"), "ctx"),
        ),
        out_specs=P(("groups", "ctx"), ("head", "sub")),
        check_vma=False,
    )
```
